32 devices in a mesh: gx: 4 (over x, core), gy: 8 (over z, y).
Axes of the slice: x: 2, y: 2, z: 4, core: 2. Of those that a mesh axis runs over, the one named last changes fastest.
Arguments:
- hidden: bfloat16 [8, 512, 1280], P('gy', 'gx'), may hold values from -6 to 6
- lengths: int32 [8], P('gy'), may hold values from 4 to 16384, as said below
- sink_kv: bfloat16 [8, 2, 4, 1024], P('gy', None, None, 'gx'), may hold values from -12 to 12
- kv_cycle: bfloat16 [8, 2, 4608, 1024], P('gy', None, None, 'gx'), may hold values from -12 to 12
- w_qkv: bfloat16 [1280, 3, 1024], P('gy', None, 'gx'), may hold values from -0.15625 to 0.15625
- s_qk: float32 [1024], P('gx'), may hold values from 0.5 to 16
- w_out: bfloat16 [1024, 1280], P('gx', 'gy'), may hold values from -0.1875 to 0.1875
- alpha_attn: float32 [1280], replicated, may hold values from 0.05 to 0.8
- w_up: bfloat16 [1280, 5120], P('gy', 'gx'), may hold values from -0.15625 to 0.15625
- w_gate: bfloat16 [1280, 5120], P('gy', 'gx'), may hold values from -0.15625 to 0.15625
- s_up: float32 [5120], P('gx'), may hold values from 0.5 to 2
- s_gate: float32 [5120], P('gx'), may hold values from 0.5 to 2
- w_down: bfloat16 [5120, 1280], P('gx', 'gy'), may hold values from -0.078125 to 0.078125
- alpha_mlp: float32 [1280], replicated, may hold values from 0.05 to 0.8
Outputs:
- new_hidden: bfloat16 [8, 512, 1280], P('gy', 'gx')
- new_cycle: bfloat16 [8, 2, 4608, 1024], P('gy', None, None, 'gx')
The draws below stay inside these ranges and needn't reach their ends.
Inputs may be any that keep to these rules, and one draw needn't show every extreme that they name: `lengths`: exactly 2 requests, chosen by the seed, have 16384 cached positions; the others have fewer than 256.
All inputs are finite; a program needn't handle non-finite values.
Results may differ from the reference program's by a relative error of at most 0.012.
The reference program's roundings to bfloat16 on the way (of `queries`, `keys_new`, `values_new`, `attended`, `after_attn` and `active`) count: a program that leaves them out, or rounds other values in their place, can miss the bound.
Values may be sent and summed in bfloat16 or wider, within the bound.
No kernel may reach another device: no remote copies, remote signals or barrier semaphores. Data moves between devices by JAX's collectives and lax.ppermute only.
A program may use at most 64 MiB of HBM per device.

```python
import math
import jax
import jax.numpy as jnp
from jax import lax

D = 1280
HD = 64
FF = 5120
HEADS = 16
HQ = 1024
NEW_TOK = 512
REQ = 8
SINK = 4
WINDOW = 4096
CYCLE = 4608
L_LONG = 16384
SHORT = 256


def scales(key):
    spread = jax.random.uniform(jax.random.fold_in(key, 1), (HEADS, HD), jnp.float32, -0.6931472, 0.6931472)
    result = jnp.exp(spread)
    return result


def cache_values(key, slots):
    scale_qk = scales(jax.random.fold_in(key, 99)).reshape(HEADS * HD)
    noise = jnp.clip(jax.random.normal(jax.random.fold_in(key, slots), (REQ, 2, slots, HEADS * HD), jnp.float32), -6.0, 6.0)
    factor = jnp.stack([scale_qk * 0.125, jnp.ones_like(scale_qk)])
    return (noise * factor[None, :, None, :]).astype(jnp.bfloat16)


def draw_lengths(key, part):
    order = jax.random.permutation(jax.random.fold_in(key, 11), REQ)
    shorter = jax.random.randint(jax.random.fold_in(key, 12), (REQ,), SINK, SHORT)
    return jnp.where(order < REQ // 4, L_LONG, shorter).astype(jnp.int32)


def draw_s_qk(key, part):
    return scales(jax.random.fold_in(key, 99)).reshape(HEADS * HD).astype(jnp.float32)


def draw_sink_kv(key, part):
    return cache_values(jax.random.fold_in(key, 21), SINK)


def draw_kv_cycle(key, part):
    return cache_values(jax.random.fold_in(key, 22), CYCLE)


def steps_of(rng, shape, split, low, top_value):
    def one(axis_at, parts):
        heights = jax.random.uniform(jax.random.fold_in(jax.random.fold_in(rng, 6), axis_at), (parts,), jnp.float32, low / len(split), top_value / len(split))
        return jnp.repeat(jnp.exp(heights), shape[axis_at] // parts).reshape((-1,) + (1,) * (len(shape) - axis_at - 1))

    loudness = one(*split[0])
    for cut in split[1:]:
        loudness = loudness * one(*cut)
    return loudness


def bell_draw(key, extent, width, bound, pieces=(), kind=jnp.bfloat16):
    array = jax.random.normal(key, extent, jnp.float32) * width
    if len(pieces) > 0:
        array = steps_of(key, extent, pieces, -0.22, 0.18) * array
    return jnp.clip(array, min=-bound, max=bound).astype(kind)


def setup_inputs(seed: int = 0) -> dict:
    splits = jax.random.split(jax.random.key(seed), 15)
    return {
        "hidden": bell_draw(splits[0], (REQ, NEW_TOK, D), 1.0, 6.0, ((0, 8), (1, 4))),
        "lengths": draw_lengths(jax.random.fold_in(splits[14], 71), 0),
        "sink_kv": draw_sink_kv(jax.random.fold_in(splits[14], 71), 0),
        "kv_cycle": draw_kv_cycle(jax.random.fold_in(splits[14], 71), 0),
        "w_qkv": bell_draw(splits[4], (D, 3, HQ), D ** -0.5, 0.15625, ((0, 8), (2, 4))),
        "s_qk": draw_s_qk(jax.random.fold_in(splits[14], 71), 0),
        "w_out": bell_draw(splits[6], (HQ, D), HQ ** -0.5, 0.1875, ((0, 4), (1, 8))),
        "alpha_attn": jnp.clip(jnp.exp(jax.random.uniform(splits[7], (D,), jnp.float32, math.log(0.05), math.log(0.8))), 0.05, 0.8),
        "w_up": bell_draw(splits[8], (D, FF), D ** -0.5, 0.15625, ((0, 8), (1, 4))),
        "w_gate": bell_draw(splits[9], (D, FF), D ** -0.5, 0.15625, ((0, 8), (1, 4))),
        "s_up": jnp.clip(jnp.exp(math.log(2.0) - 1.3862944 * jax.random.uniform(splits[10], (FF,), jnp.float32) ** steps_of(splits[10], (FF,), ((0, 4),), -0.2, 0.2)), 0.5, 2.0),
        "s_gate": jnp.clip(jnp.exp(math.log(2.0) - 1.3862944 * jax.random.uniform(splits[11], (FF,), jnp.float32) ** steps_of(splits[11], (FF,), ((0, 4),), -0.2, 0.2)), 0.5, 2.0),
        "w_down": bell_draw(splits[12], (FF, D), FF ** -0.5, 0.078125, ((0, 4), (1, 8))),
        "alpha_mlp": jnp.clip(jnp.exp(jax.random.uniform(splits[13], (D,), jnp.float32, math.log(0.05), math.log(0.8))), 0.05, 0.8),
    }


def rms_unit(values):
    return values * lax.rsqrt(lax.optimization_barrier(jnp.mean(values * values, axis=-1, keepdims=True)) + 1e-06)

def head_unit(values):
    return values * lax.rsqrt(lax.optimization_barrier(jnp.sum(values * values, axis=-1, keepdims=True)) + 1e-06)

def slot_positions(length, slot_ids):
    lagging = length + NEW_TOK - 1 - SINK - slot_ids
    filled = lagging >= 0
    wrapped = jnp.where(filled, lagging, 0) // CYCLE
    return (SINK + slot_ids + CYCLE * wrapped, filled)

def reference(hidden, lengths, sink_kv, kv_cycle, w_qkv, s_qk, w_out, alpha_attn, w_up, w_gate, s_up, s_gate, w_down, alpha_mlp):
    scale_qk = s_qk.reshape(HEADS, HD)
    factor = math.sqrt(HD)

    def one_request(operands):
        tokens, length, sink_rows, cached = operands
        projected = jnp.dot(tokens, w_qkv.reshape(D, 3 * HQ), preferred_element_type=jnp.float32).reshape(NEW_TOK, 3, HEADS, HD)
        queries = (head_unit(projected[:, 0]) * scale_qk).astype(jnp.bfloat16)
        keys_new = (head_unit(projected[:, 1]) * scale_qk).astype(jnp.bfloat16)
        values_new = projected[:, 2].astype(jnp.bfloat16)
        start_slot = (length - SINK) % CYCLE
        targets = (start_slot + jnp.arange(NEW_TOK, dtype=jnp.int32)) % CYCLE
        updated = cached.at[0, targets].set(keys_new.reshape(NEW_TOK, HQ))
        updated = updated.at[1, targets].set(values_new.reshape(NEW_TOK, HQ))
        positions, filled = slot_positions(length, jnp.arange(CYCLE, dtype=jnp.int32))
        moments = length + jnp.arange(NEW_TOK, dtype=jnp.int32)
        visible = filled[None, :] & (positions[None, :] <= moments[:, None]) & (positions[None, :] > moments[:, None] - WINDOW)
        visible = jnp.concatenate([jnp.ones((NEW_TOK, SINK), jnp.int32) > 0, visible], axis=1)
        all_keys = jnp.concatenate([sink_rows[0], updated[0]], axis=0).reshape(SINK + CYCLE, HEADS, HD)
        all_values = jnp.concatenate([sink_rows[1], updated[1]], axis=0).reshape(SINK + CYCLE, HEADS, HD)
        scores = jnp.einsum('qhd,khd->qhk', queries.astype(jnp.float32), all_keys.astype(jnp.float32)) * factor
        scores = jnp.where(visible[:, None, :], scores, -1e+30)
        highest = lax.optimization_barrier(jnp.max(scores, axis=-1, keepdims=True))
        weights = jnp.where(visible[:, None, :], jnp.exp(scores - highest), 0.0)
        totals = lax.optimization_barrier(jnp.sum(weights, axis=-1))
        rounded = lax.optimization_barrier(weights.astype(jnp.bfloat16)).astype(jnp.float32)
        gathered = jnp.einsum('qhk,khd->qhd', rounded, all_values.astype(jnp.float32))
        attended = (gathered / totals[:, :, None]).astype(jnp.bfloat16).reshape(NEW_TOK, HQ)
        attn_mixed = jnp.dot(attended, w_out, preferred_element_type=jnp.float32)
        residual = tokens.astype(jnp.float32)
        after_attn = rms_unit(residual + alpha_attn * (rms_unit(attn_mixed) - residual)).astype(jnp.bfloat16)
        up_branch = jnp.dot(after_attn, w_up, preferred_element_type=jnp.float32) * s_up
        gate_branch = jnp.dot(after_attn, w_gate, preferred_element_type=jnp.float32) * s_gate
        active = (up_branch * jax.nn.silu(gate_branch)).astype(jnp.bfloat16)
        lowered = jnp.dot(active, w_down, preferred_element_type=jnp.float32)
        after_wide = after_attn.astype(jnp.float32)
        result = rms_unit(after_wide + alpha_mlp * (rms_unit(lowered) - after_wide)).astype(jnp.bfloat16)
        return (result, updated)
    new_hidden, new_cycle = lax.map(one_request, (hidden, lengths, sink_kv, kv_cycle))
    return (new_hidden, new_cycle)
```

```python
import functools
import math

import jax
import jax.numpy as jnp
from jax import lax
from jax.experimental import pallas as pl
from jax.experimental.pallas import tpu as pltpu
from jax.sharding import PartitionSpec as P

HD = 64
SINK = 4
WINDOW = 4096
SHORT_KEYS = 768
CHUNK = 512
NEG = -1e30
VMEM = pl.BlockSpec(memory_space=pltpu.VMEM)
SMEM = pl.BlockSpec(memory_space=pltpu.SMEM)
ANY = pl.BlockSpec(memory_space=pl.ANY)


def rms_unit(values):
    return values * lax.rsqrt(jnp.mean(values * values, axis=-1, keepdims=True) + 1e-06)


def kernel_params(mib=56):
    return pltpu.CompilerParams(vmem_limit_bytes=mib << 20)


class Layout:
    def __init__(self, gx, gy):
        self.nc = 2
        self.nx = gx // 2
        self.ny = self.nx
        self.nz = gy // self.ny
        mine_x, mine_y = lax.axis_index("gx"), lax.axis_index("gy")
        self.x, self.c = mine_x // self.nc, mine_x % self.nc
        self.z, self.y = mine_y // self.ny, mine_y % self.ny

    def from_z(self, value):
        pairs = [
            (z * self.ny + y, (z - 1) % self.nz * self.ny + y)
            for z in range(self.nz)
            for y in range(self.ny)
        ]
        return lax.ppermute(value, "gy", pairs)

    def from_y(self, value):
        pairs = [
            (z * self.ny + y, z * self.ny + (y - 1) % self.ny)
            for z in range(self.nz)
            for y in range(self.ny)
        ]
        return lax.ppermute(value, "gy", pairs)

    def to_x(self, value, step):
        pairs = [
            (x * 2 + c, (x + step) % self.nx * 2 + c) for x in range(self.nx) for c in range(2)
        ]
        return lax.ppermute(value, "gx", pairs)

    def swap_core(self, value):
        pairs = [(x * 2 + c, x * 2 + 1 - c) for x in range(self.nx) for c in range(2)]
        return lax.ppermute(value, "gx", pairs)

    def gather(self, shard):
        pieces = []
        held = shard
        for k in range(self.nz):
            if k:
                held = self.from_z(held)
            side = held
            for j in range(self.ny):
                if j:
                    side = self.from_y(side)
                pieces.append(side)
        return pieces

    def turned_source(self, width):
        place = lax.broadcasted_iota(jnp.int32, (1, width), 1)
        part = width // (self.nz * self.ny)
        piece, inside = place // part, place % part
        k, j = piece // self.ny, piece % self.ny
        block = (self.z + k) % self.nz * self.ny + (self.y + j) % self.ny
        return block * part + inside

    def turn_vector(self, vector):
        rows = vector.reshape(self.nz, -1)
        rows = lax.dynamic_slice_in_dim(jnp.concatenate([rows, rows]), self.z, self.nz, 0)
        rows = rows.reshape(self.nz, self.ny, -1)
        rows = jnp.concatenate([rows, rows], axis=1)
        return lax.dynamic_slice_in_dim(rows, self.y, self.ny, 1).reshape(-1)

    def gather_rows(self, own):
        blocks = []
        for d in range(self.nx):
            block = self.to_x(own, d) if d else own
            blocks += [block, self.swap_core(block)]
        return jnp.concatenate(blocks, axis=0)

    def scatter_rows(self, partial, own_rows):
        wide = partial.reshape(self.nx, 2, own_rows, partial.shape[-1])
        other = self.swap_core(wide[:, 1])
        summed = wide[:, 0].astype(jnp.float32) + other.astype(jnp.float32)
        total = summed[0]
        for d in range(1, self.nx):
            total += self.to_x(summed[d].astype(jnp.bfloat16), -d).astype(jnp.float32)
        return total


def joined(refs, *index):
    return jnp.concatenate([ref[index] if index else ref[...] for ref in refs], axis=0)


def qkv_kernel(count, own_rows, scalars, rows_ref, scale_ref, cycle_in, *rest):
    pieces, (query_ref, cycle_ref, window, fresh, sems) = rest[:count], rest[count:]
    del cycle_in
    length, x, c, nx = scalars[0], scalars[1], scalars[2], scalars[3]
    new_count, local_cols = query_ref.shape
    cycle_size = cycle_ref.shape[1]
    span = window.shape[1]
    start = lax.rem(length - SINK, cycle_size)
    base = jnp.minimum(start // 16 * 16, cycle_size - span)
    base = pl.multiple_of(base, 16)
    loads = [
        pltpu.make_async_copy(cycle_ref.at[i, pl.ds(base, span), :], window.at[i], sems.at[i])
        for i in range(2)
    ]
    for load in loads:
        load.start()
    rows = rows_ref[...]
    lane_head = lax.broadcasted_iota(jnp.int32, (1, local_cols), 1) // HD

    def unit(values):
        squares = values * values
        total = jnp.zeros_like(values)
        for head in range(local_cols // HD):
            picked = lane_head == head
            part = jnp.sum(jnp.where(picked, squares, 0.0), axis=-1, keepdims=True)
            total = jnp.where(picked, part, total)
        return values * lax.rsqrt(total + 1e-06) * scale_ref[...]

    def project(which):
        return jnp.dot(rows, joined(pieces, which), preferred_element_type=jnp.float32)

    queries = unit(project(0)).astype(jnp.bfloat16)
    query_ref[...] = (queries.astype(jnp.float32) * math.sqrt(HD)).astype(jnp.bfloat16)
    fresh[0] = unit(project(1)).astype(jnp.bfloat16)
    fresh[1] = project(2).astype(jnp.bfloat16)
    row = lax.broadcasted_iota(jnp.int32, (1, new_count), 1)
    block, inside = row // own_rows, row % own_rows
    from_x = lax.rem(x - block // 2 + nx, nx)
    from_c = jnp.where(block % 2 == 1, 1 - c, c)
    token = (from_x * 2 + from_c) * own_rows + inside
    target = token + (start - base)
    slot = lax.broadcasted_iota(jnp.int32, (span, 1), 0)
    pick = (slot == target).astype(jnp.float32).astype(jnp.bfloat16)
    offset = slot - (start - base)
    replaced = (offset >= 0) & (offset < new_count)
    for i in range(2):
        loads[i].wait()
        moved = jnp.dot(pick, fresh[i], preferred_element_type=jnp.float32)
        window[i] = jnp.where(replaced, moved, window[i].astype(jnp.float32)).astype(jnp.bfloat16)
        store = pltpu.make_async_copy(
            window.at[i], cycle_ref.at[i, pl.ds(base, span), :], sems.at[i]
        )
        store.start()
    for i in range(2):
        pltpu.make_async_copy(
            window.at[i], cycle_ref.at[i, pl.ds(base, span), :], sems.at[i]
        ).wait()


def attention_kernel(own_rows, scalars, query_ref, cycle_ref, sink_ref, out_ref, scores, bias):
    length, x, c, nx = scalars[0], scalars[1], scalars[2], scalars[3]
    new_count, lanes = query_ref.shape
    cycle_size = cycle_ref.shape[1]
    lane_head = lax.broadcasted_iota(jnp.int32, (1, lanes), 1) // HD
    sink_lane = lax.broadcasted_iota(jnp.int32, (1, sink_ref.shape[1]), 1)
    sink_bias = jnp.where(sink_lane < SINK, 0.0, NEG)
    contract = (((1,), (1,)), ((), ()))

    def run(keys):
        sizes = [min(CHUNK, keys - at) for at in range(0, keys, CHUNK)]
        starts = [CHUNK * n for n in range(len(sizes))]

        def tile(i, _):
            from_x = lax.rem(x - i // 2 + nx, nx)
            from_c = jnp.where(i % 2 == 1, 1 - c, c)
            first = (from_x * 2 + from_c) * own_rows
            at = pl.multiple_of(i * own_rows, own_rows)
            queries = query_ref[pl.ds(at, own_rows), :]
            moment = first + lax.broadcasted_iota(jnp.int32, (own_rows, 1), 0)
            for begin, size in zip(starts, sizes):
                slot = begin + lax.broadcasted_iota(jnp.int32, (1, size), 1)
                lagging = length + new_count - 1 - SINK - slot
                turn = cycle_size * (jnp.maximum(lagging, 0) // cycle_size)
                ahead = jnp.where(lagging >= 0, SINK + slot + turn - length, 1 << 20)
                lag = moment - ahead
                seen = (lag >= 0) & (lag < WINDOW)
                bias[:, begin : begin + size] = jnp.where(seen, 0.0, NEG)
            result = jnp.zeros((own_rows, lanes), jnp.float32)
            for head in range(lanes // HD):
                mine = lane_head == head
                picked = jnp.where(mine, queries.astype(jnp.float32), 0.0).astype(jnp.bfloat16)
                sink_scores = (
                    lax.dot_general(
                        picked, sink_ref[0], contract, preferred_element_type=jnp.float32
                    )
                    + sink_bias
                )
                highest = jnp.max(sink_scores, axis=-1, keepdims=True)
                for begin, size in zip(starts, sizes):
                    part = lax.dot_general(
                        picked,
                        cycle_ref[0, begin : begin + size, :],
                        contract,
                        preferred_element_type=jnp.float32,
                    )
                    part = part + bias[:, begin : begin + size]
                    scores[:, begin : begin + size] = part
                    highest = jnp.maximum(highest, jnp.max(part, axis=-1, keepdims=True))
                weights = jnp.exp(sink_scores - highest)
                total = jnp.sum(weights, axis=-1, keepdims=True)
                summed = jnp.dot(
                    weights.astype(jnp.bfloat16), sink_ref[1], preferred_element_type=jnp.float32
                )
                for begin, size in zip(starts, sizes):
                    weights = jnp.exp(scores[:, begin : begin + size] - highest)
                    total += jnp.sum(weights, axis=-1, keepdims=True)
                    summed += jnp.dot(
                        weights.astype(jnp.bfloat16),
                        cycle_ref[1, begin : begin + size, :],
                        preferred_element_type=jnp.float32,
                    )
                result = jnp.where(mine, summed / total, result)
            out_ref[pl.ds(at, own_rows), :] = result.astype(jnp.bfloat16)
            return 0

        lax.fori_loop(0, new_count // own_rows, tile, 0)

    few = length + new_count - SINK <= SHORT_KEYS

    @pl.when(few)
    def _():
        run(SHORT_KEYS)

    @pl.when(jnp.logical_not(few))
    def _():
        run(cycle_size)


def mix_kernel(count, parts, *refs):
    attended, pieces, out_ref = refs[:parts], refs[parts : parts + count], refs[parts + count]
    wide = jnp.concatenate([ref[...] for ref in attended], axis=1)
    out_ref[...] = lax.dot_general(
        wide, joined(pieces), (((1,), (1,)), ((), ())), preferred_element_type=jnp.float32
    ).astype(jnp.bfloat16)


def hidden_units_kernel(count, rows_ref, up_scale, gate_scale, *refs):
    up_pieces, gate_pieces, out_ref = refs[:count], refs[count : 2 * count], refs[2 * count]
    rows = rows_ref[...]
    up = jnp.dot(rows, joined(up_pieces), preferred_element_type=jnp.float32) * up_scale[...]
    gate = jnp.dot(rows, joined(gate_pieces), preferred_element_type=jnp.float32) * gate_scale[...]
    out_ref[...] = (up * (gate / (1.0 + jnp.exp(-gate)))).astype(jnp.bfloat16)


def lower_kernel(count, active_ref, *refs):
    pieces, out_ref, held = refs[:count], refs[count], refs[count + 1]
    part = pieces[0].shape[0]
    for n in range(count):
        held[n * part : (n + 1) * part, :] = pieces[n][...]
    out_ref[...] = lax.dot_general(
        active_ref[...], held[...], (((1,), (1,)), ((), ())), preferred_element_type=jnp.float32
    ).astype(jnp.bfloat16)


def per_device(
    axes,
    hidden,
    lengths,
    sink_kv,
    kv_cycle,
    w_qkv,
    s_qk,
    w_out,
    alpha_attn,
    w_up,
    w_gate,
    s_up,
    s_gate,
    w_down,
    alpha_mlp,
):
    here = Layout(*axes)
    _, own_rows, model_width = hidden.shape
    new_count = own_rows * axes[0]
    local_cols = s_qk.shape[0]
    cycle_size = kv_cycle.shape[2]
    count = axes[1]
    units = s_up.shape[0]
    lanes = min(128, local_cols)
    parts = local_cols // lanes
    span = min(new_count + 16, cycle_size)

    source = here.turned_source(model_width)
    turn = (lax.broadcasted_iota(jnp.int32, (model_width, 1), 0) == source).astype(jnp.bfloat16)
    own_hidden = jnp.dot(hidden[0], turn, preferred_element_type=jnp.float32).astype(jnp.bfloat16)
    rows = here.gather_rows(own_hidden)
    step_attn, step_mlp = here.turn_vector(alpha_attn), here.turn_vector(alpha_mlp)

    qkv_pieces = here.gather(w_qkv.transpose(1, 0, 2))
    out_pieces = here.gather(w_out.T)
    up_pieces = here.gather(w_up)
    gate_pieces = here.gather(w_gate)
    down_pieces = here.gather(w_down.T)

    scalars = jnp.stack([lengths[0], here.x, here.c, jnp.int32(here.nx)])
    queries, new_cycle = pl.pallas_call(
        functools.partial(qkv_kernel, count, own_rows),
        out_shape=(
            jax.ShapeDtypeStruct((new_count, local_cols), jnp.bfloat16),
            jax.ShapeDtypeStruct(kv_cycle.shape[1:], jnp.bfloat16),
        ),
        in_specs=[SMEM, VMEM, VMEM, ANY] + [VMEM] * count,
        out_specs=(VMEM, ANY),
        scratch_shapes=[
            pltpu.VMEM((2, span, local_cols), jnp.bfloat16),
            pltpu.VMEM((2, new_count, local_cols), jnp.bfloat16),
            pltpu.SemaphoreType.DMA((2,)),
        ],
        input_output_aliases={3: 1},
        compiler_params=kernel_params(),
        name="qkv",
    )(scalars, rows, s_qk[None], kv_cycle[0], *qkv_pieces)

    sinks = jnp.pad(sink_kv[0], ((0, 0), (0, 128 - SINK), (0, 0)))
    attended = [
        pl.pallas_call(
            functools.partial(attention_kernel, own_rows),
            grid=(1,),
            out_shape=jax.ShapeDtypeStruct((new_count, lanes), jnp.bfloat16),
            in_specs=[
                SMEM,
                pl.BlockSpec((new_count, lanes), lambda _, part=part: (0, part)),
                pl.BlockSpec((2, cycle_size, lanes), lambda _, part=part: (0, 0, part)),
                pl.BlockSpec((2, 128, lanes), lambda _, part=part: (0, 0, part)),
            ],
            out_specs=pl.BlockSpec((new_count, lanes), lambda _: (0, 0)),
            scratch_shapes=[
                pltpu.VMEM((own_rows, cycle_size), jnp.float32),
                pltpu.VMEM((own_rows, cycle_size), jnp.float32),
            ],
            compiler_params=kernel_params(),
            name=f"attention{part}",
        )(scalars, queries, new_cycle, sinks)
        for part in range(parts)
    ]

    mixed = pl.pallas_call(
        functools.partial(mix_kernel, count, parts),
        out_shape=jax.ShapeDtypeStruct((new_count, model_width), jnp.bfloat16),
        in_specs=[VMEM] * (parts + count),
        out_specs=VMEM,
        compiler_params=kernel_params(),
        name="mix",
    )(*attended, *out_pieces)
    summed = here.scatter_rows(mixed, own_rows)
    residual = own_hidden.astype(jnp.float32)
    after_own = rms_unit(residual + step_attn * (rms_unit(summed) - residual)).astype(jnp.bfloat16)
    after_all = here.gather_rows(after_own)

    tile = 256 if units % 256 == 0 else 128
    piece_rows = w_up.shape[0]
    active = pl.pallas_call(
        functools.partial(hidden_units_kernel, count),
        grid=(units // tile,),
        out_shape=jax.ShapeDtypeStruct((new_count, units), jnp.bfloat16),
        in_specs=[pl.BlockSpec((new_count, model_width), lambda n: (0, 0))]
        + [pl.BlockSpec((1, tile), lambda n: (0, n))] * 2
        + [pl.BlockSpec((piece_rows, tile), lambda n: (0, n))] * (2 * count),
        out_specs=pl.BlockSpec((new_count, tile), lambda n: (0, n)),
        compiler_params=kernel_params(),
        name="hidden_units",
    )(after_all, s_up[None], s_gate[None], *up_pieces, *gate_pieces)
    lowered = pl.pallas_call(
        functools.partial(lower_kernel, count),
        out_shape=jax.ShapeDtypeStruct((new_count, model_width), jnp.bfloat16),
        in_specs=[VMEM] * (1 + count),
        out_specs=VMEM,
        scratch_shapes=[pltpu.VMEM((model_width, units), jnp.bfloat16)],
        compiler_params=kernel_params(),
        name="lower",
    )(active, *down_pieces)
    lowered_own = here.scatter_rows(lowered, own_rows)
    own_wide = after_own.astype(jnp.float32)
    result = rms_unit(own_wide + step_mlp * (rms_unit(lowered_own) - own_wide)).astype(jnp.bfloat16)
    result = lax.dot_general(
        result, turn, (((1,), (1,)), ((), ())), preferred_element_type=jnp.float32
    ).astype(jnp.bfloat16)
    return (result[None], new_cycle[None])


def solution(mesh):
    axes = (mesh.shape["gx"], mesh.shape["gy"])
    return jax.shard_map(
        functools.partial(per_device, axes),
        mesh=mesh,
        in_specs=(
            P("gy", "gx", None),
            P("gy"),
            P("gy", None, None, "gx"),
            P("gy", None, None, "gx"),
            P("gy", None, "gx"),
            P("gx"),
            P("gx", "gy"),
            P(),
            P("gy", "gx"),
            P("gy", "gx"),
            P("gx"),
            P("gx"),
            P("gx", "gy"),
            P(),
        ),
        out_specs=(P("gy", "gx", None), P("gy", None, None, "gx")),
        check_vma=False,
    )
```

```python
import functools
import math

import jax
import jax.numpy as jnp
from jax import lax
from jax.experimental import pallas as pl
from jax.experimental.pallas import tpu as pltpu
from jax.sharding import PartitionSpec as P


HD = 64
SINK = 4
WINDOW = 4096
SHORT_KEYS = 768
CHUNK = 512
NEG = -1e30
FIXED = 4
VMEM = pl.BlockSpec(memory_space=pltpu.VMEM)
SMEM = pl.BlockSpec(memory_space=pltpu.SMEM)
ANY = pl.BlockSpec(memory_space=pl.ANY)
PARAMS = pltpu.CompilerParams(vmem_limit_bytes=56 << 20)


def rms_unit(values):
    return values * lax.rsqrt(jnp.mean(values * values, axis=-1, keepdims=True) + 1e-06)


class Layout:
    def __init__(self, gx, gy):
        self.plain = (gx, gy) != (4, 8)
        self.nx = gx // 2
        self.ny = self.nx
        self.nz = gy // self.ny
        mine_x, mine_y = lax.axis_index("gx"), lax.axis_index("gy")
        self.x, self.c = mine_x // 2, mine_x % 2
        self.z, self.y = mine_y // self.ny, mine_y % self.ny

    def from_z(self, value):
        pairs = [
            (z * self.ny + y, (z - 1) % self.nz * self.ny + y)
            for z in range(self.nz)
            for y in range(self.ny)
        ]
        return lax.ppermute(value, "gy", pairs)

    def from_y(self, value):
        pairs = [
            (z * self.ny + y, z * self.ny + (y - 1) % self.ny)
            for z in range(self.nz)
            for y in range(self.ny)
        ]
        return lax.ppermute(value, "gy", pairs)

    def to_x(self, value, step):
        pairs = [
            (x * 2 + c, (x + step) % self.nx * 2 + c) for x in range(self.nx) for c in range(2)
        ]
        return lax.ppermute(value, "gx", pairs)

    def swap_core(self, value):
        pairs = [(x * 2 + c, x * 2 + 1 - c) for x in range(self.nx) for c in range(2)]
        return lax.ppermute(value, "gx", pairs)

    def blocks(self):
        if self.plain:
            return [jnp.int32(0)]
        return [
            (self.z + k) % self.nz * self.ny + (self.y + j) % self.ny
            for k in range(self.nz)
            for j in range(self.ny)
        ]

    def gather(self, shard):
        if self.plain:
            return [(lax.all_gather(shard, "gy", axis=shard.ndim - 2, tiled=True), ())]
        pieces = []
        held = shard
        for k in range(self.nz):
            if k:
                held = self.from_z(held)
            side = held
            for j in range(self.ny):
                if j:
                    side = self.from_y(side)
                pieces.append((side, ()))
        return pieces

    def gather_y_first(self, shard):
        if self.plain:
            return self.gather(shard)
        held = [shard]
        for _ in range(1, self.ny):
            held.append(self.from_y(held[-1]))
        held = jnp.stack(held)
        pieces = []
        for k in range(self.nz):
            if k:
                held = self.from_z(held)
            pieces += [(held, (j,)) for j in range(self.ny)]
        return pieces

    def core_sum(self, halves):
        kept, sent = halves
        return kept.astype(jnp.float32) + self.swap_core(sent).astype(jnp.float32)


def pieces_of(pieces):
    arrays, spots = [], []
    for array, index in pieces:
        known = [n for n, other in enumerate(arrays) if other is array]
        if not known:
            arrays.append(array)
        spots.append((known[0] if known else len(arrays) - 1, index))
    return arrays, tuple(spots)


def place(scalars, refs, spots, held, plane=(), lane=0):
    for n, (number, index) in enumerate(spots):
        value = refs[number][index + plane]
        rows, lanes = value.shape
        at = pl.multiple_of(scalars[FIXED + n] * rows, 16)
        held[pl.ds(at, rows), lane : lane + lanes] = value


def split_rows(value, kept_ref, sent_ref, own_rows):
    for d in range(value.shape[0] // (2 * own_rows)):
        at = slice(d * own_rows, (d + 1) * own_rows)
        kept_ref[at, :] = value[2 * d * own_rows : (2 * d + 1) * own_rows]
        sent_ref[at, :] = value[(2 * d + 1) * own_rows : (2 * d + 2) * own_rows]


def stage_kernel(source, target):
    target[...] = source[...]


def qkv_kernel(spots, count, blocks, own_rows, scalars, scale_ref, cycle_in, *rest):
    pieces, row_refs = rest[:count], rest[count : count + blocks]
    query_ref, cycle_ref, window, fresh, held, sems = rest[count + blocks :]
    del cycle_in
    length, x, c, nx = scalars[0], scalars[1], scalars[2], scalars[3]
    new_count, local_cols = query_ref.shape
    cycle_size = cycle_ref.shape[1]
    span = window.shape[1]
    start = lax.rem(length - SINK, cycle_size)
    base = jnp.minimum(start // 16 * 16, cycle_size - span)
    base = pl.multiple_of(base, 16)
    loads = [
        pltpu.make_async_copy(cycle_ref.at[i, pl.ds(base, span), :], window.at[i], sems.at[i])
        for i in range(2)
    ]
    for load in loads:
        load.start()
    rows = jnp.concatenate([ref[...] for ref in row_refs], axis=0)
    lane_head = lax.broadcasted_iota(jnp.int32, (1, local_cols), 1) // HD

    def unit(values):
        squares = values * values
        total = jnp.zeros_like(values)
        for head in range(local_cols // HD):
            picked = lane_head == head
            part = jnp.sum(jnp.where(picked, squares, 0.0), axis=-1, keepdims=True)
            total = jnp.where(picked, part, total)
        return values * lax.rsqrt(total + 1e-06) * scale_ref[...]

    def project(which):
        place(scalars, pieces, spots, held.at[which], (which,))
        return jnp.dot(rows, held[which], preferred_element_type=jnp.float32)

    queries = unit(project(0)).astype(jnp.bfloat16)
    query_ref[...] = (queries.astype(jnp.float32) * math.sqrt(HD)).astype(jnp.bfloat16)
    fresh[0] = unit(project(1)).astype(jnp.bfloat16)
    fresh[1] = project(2).astype(jnp.bfloat16)
    row = lax.broadcasted_iota(jnp.int32, (1, new_count), 1)
    block, inside = row // own_rows, row % own_rows
    from_x = lax.rem(x - block // 2 + nx, nx)
    from_c = jnp.where(block % 2 == 1, 1 - c, c)
    token = (from_x * 2 + from_c) * own_rows + inside
    target = token + (start - base)
    slot = lax.broadcasted_iota(jnp.int32, (span, 1), 0)
    pick = (slot == target).astype(jnp.float32).astype(jnp.bfloat16)
    offset = slot - (start - base)
    replaced = (offset >= 0) & (offset < new_count)
    stores = []
    for i in range(2):
        loads[i].wait()
        moved = jnp.dot(pick, fresh[i], preferred_element_type=jnp.float32)
        window[i] = jnp.where(replaced, moved, window[i].astype(jnp.float32)).astype(jnp.bfloat16)
        store = pltpu.make_async_copy(
            window.at[i], cycle_ref.at[i, pl.ds(base, span), :], sems.at[i]
        )
        store.start()
        stores.append(store)
    for store in stores:
        store.wait()


def attention_kernel(own_rows, scalars, query_ref, cycle_ref, sink_ref, out_ref, scores, bias):
    length, x, c, nx = scalars[0], scalars[1], scalars[2], scalars[3]
    new_count, lanes = query_ref.shape
    cycle_size = cycle_ref.shape[1]
    lane_head = lax.broadcasted_iota(jnp.int32, (1, lanes), 1) // HD
    sink_lane = lax.broadcasted_iota(jnp.int32, (1, sink_ref.shape[1]), 1)
    sink_bias = jnp.where(sink_lane < SINK, 0.0, NEG)
    contract = (((1,), (1,)), ((), ()))

    def run(keys):
        sizes = [min(CHUNK, keys - at) for at in range(0, keys, CHUNK)]
        starts = [CHUNK * n for n in range(len(sizes))]

        def tile(i, _):
            from_x = lax.rem(x - i // 2 + nx, nx)
            from_c = jnp.where(i % 2 == 1, 1 - c, c)
            first = (from_x * 2 + from_c) * own_rows
            at = pl.multiple_of(i * own_rows, own_rows)
            queries = query_ref[pl.ds(at, own_rows), :]
            moment = first + lax.broadcasted_iota(jnp.int32, (own_rows, 1), 0)
            for begin, size in zip(starts, sizes):
                slot = begin + lax.broadcasted_iota(jnp.int32, (1, size), 1)
                lagging = length + new_count - 1 - SINK - slot
                turn = cycle_size * (jnp.maximum(lagging, 0) // cycle_size)
                ahead = jnp.where(lagging >= 0, SINK + slot + turn - length, 1 << 20)
                lag = moment - ahead
                seen = (lag >= 0) & (lag < WINDOW)
                bias[:, begin : begin + size] = jnp.where(seen, 0.0, NEG)
            result = jnp.zeros((own_rows, lanes), jnp.float32)
            for head in range(lanes // HD):
                mine = lane_head == head
                picked = jnp.where(mine, queries.astype(jnp.float32), 0.0).astype(jnp.bfloat16)
                sink_scores = (
                    lax.dot_general(
                        picked, sink_ref[0], contract, preferred_element_type=jnp.float32
                    )
                    + sink_bias
                )
                highest = jnp.max(sink_scores, axis=-1, keepdims=True)
                for begin, size in zip(starts, sizes):
                    part = lax.dot_general(
                        picked,
                        cycle_ref[0, begin : begin + size, :],
                        contract,
                        preferred_element_type=jnp.float32,
                    )
                    part = part + bias[:, begin : begin + size]
                    scores[:, begin : begin + size] = part
                    highest = jnp.maximum(highest, jnp.max(part, axis=-1, keepdims=True))
                weights = jnp.exp(sink_scores - highest)
                total = jnp.sum(weights, axis=-1, keepdims=True)
                summed = jnp.dot(
                    weights.astype(jnp.bfloat16), sink_ref[1], preferred_element_type=jnp.float32
                )
                for begin, size in zip(starts, sizes):
                    weights = jnp.exp(scores[:, begin : begin + size] - highest)
                    total += jnp.sum(weights, axis=-1, keepdims=True)
                    summed += jnp.dot(
                        weights.astype(jnp.bfloat16),
                        cycle_ref[1, begin : begin + size, :],
                        preferred_element_type=jnp.float32,
                    )
                result = jnp.where(mine, summed / total, result)
            out_ref[pl.ds(at, own_rows), :] = result.astype(jnp.bfloat16)
            return 0

        lax.fori_loop(0, new_count // own_rows, tile, 0)

    few = length + new_count - SINK <= SHORT_KEYS

    @pl.when(few)
    def _():
        run(SHORT_KEYS)

    @pl.when(jnp.logical_not(few))
    def _():
        run(cycle_size)


def mix_kernel(spots, count, parts, own_rows, rows, scalars, *refs):
    attended, pieces = refs[:parts], refs[parts : parts + count]
    kept_ref, sent_ref, held = refs[parts + count :]
    place(scalars, pieces, spots, held)
    wide = jnp.concatenate([ref[rows, :] for ref in attended], axis=1)
    mixed = lax.dot_general(
        wide, held[...], (((1,), (1,)), ((), ())), preferred_element_type=jnp.float32
    ).astype(jnp.bfloat16)
    split_rows(mixed, kept_ref, sent_ref, own_rows)


def units_kernel(spots, count, blocks, scalars, up_scale, gate_scale, *refs):
    pieces, row_refs = refs[:count], refs[count : count + blocks]
    out_ref, held = refs[count + blocks :]
    rows = jnp.concatenate([ref[...] for ref in row_refs], axis=0)
    for plane in range(2):
        place(scalars, pieces, spots, held.at[plane], (plane,))
    up = jnp.dot(rows, held[0], preferred_element_type=jnp.float32) * up_scale[...]
    gate = jnp.dot(rows, held[1], preferred_element_type=jnp.float32) * gate_scale[...]
    out_ref[...] = (up * (gate / (1.0 + jnp.exp(-gate)))).astype(jnp.bfloat16)


def lower_kernel(spots, counts, own_rows, rows, scalars, active_ref, *refs):
    kept_ref, sent_ref, held = refs[sum(counts) :]
    lane = 0
    for n, count in enumerate(counts):
        pieces = refs[sum(counts[:n]) : sum(counts[: n + 1])]
        place(scalars, pieces, spots[n], held, lane=lane)
        lane += pieces[0].shape[-1]
    lowered = lax.dot_general(
        active_ref[rows, :], held[...], (((1,), (1,)), ((), ())), preferred_element_type=jnp.float32
    ).astype(jnp.bfloat16)
    split_rows(lowered, kept_ref, sent_ref, own_rows)


def per_device(
    axes,
    hidden,
    lengths,
    sink_kv,
    kv_cycle,
    w_qkv,
    s_qk,
    w_out,
    alpha_attn,
    w_up,
    w_gate,
    s_up,
    s_gate,
    w_down,
    alpha_mlp,
):
    here = Layout(*axes)
    _, own_rows, model_width = hidden.shape
    nx, blocks = here.nx, axes[0]
    new_count = own_rows * blocks
    local_cols = s_qk.shape[0]
    cycle_size = kv_cycle.shape[2]
    units = s_up.shape[0]
    lanes = min(128, local_cols)
    parts = local_cols // lanes
    span = min(new_count + 16, cycle_size)
    chunk = cycle_size // 9

    row_blocks = []
    for d in range(nx):
        block = here.to_x(hidden[0], d) if d else hidden[0]
        row_blocks += [block, here.swap_core(block)]

    qkv_arrays, qkv_spots = pieces_of(here.gather(w_qkv.transpose(1, 0, 2)))
    out_arrays, out_spots = pieces_of(here.gather_y_first(w_out.T))
    gated_arrays, gated_spots = pieces_of(here.gather(jnp.stack([w_up, w_gate])))
    lower_t = w_down.T
    half = units // 2
    first_arrays, first_spots = pieces_of(here.gather_y_first(lower_t[:, :half]))
    second_arrays, second_spots = pieces_of(here.gather(lower_t[:, half:]))

    scalars = jnp.stack([lengths[0], here.x, here.c, jnp.int32(nx), *here.blocks()])
    staged = pl.pallas_call(
        stage_kernel,
        grid=(9,),
        out_shape=jax.ShapeDtypeStruct(kv_cycle.shape[1:], jnp.bfloat16),
        in_specs=[pl.BlockSpec((2, chunk, local_cols), lambda n: (0, n, 0))],
        out_specs=pl.BlockSpec((2, chunk, local_cols), lambda n: (0, n, 0)),
        compiler_params=PARAMS,
        name="stage",
    )(kv_cycle[0])
    queries, new_cycle = pl.pallas_call(
        functools.partial(qkv_kernel, qkv_spots, len(qkv_arrays), blocks, own_rows),
        out_shape=(
            jax.ShapeDtypeStruct((new_count, local_cols), jnp.bfloat16),
            jax.ShapeDtypeStruct(kv_cycle.shape[1:], jnp.bfloat16),
        ),
        in_specs=[SMEM, VMEM, ANY] + [VMEM] * (len(qkv_arrays) + blocks),
        out_specs=(VMEM, ANY),
        scratch_shapes=[
            pltpu.VMEM((2, span, local_cols), jnp.bfloat16),
            pltpu.VMEM((2, new_count, local_cols), jnp.bfloat16),
            pltpu.VMEM((3, model_width, local_cols), jnp.bfloat16),
            pltpu.SemaphoreType.DMA((2,)),
        ],
        input_output_aliases={2: 1},
        compiler_params=PARAMS,
        name="qkv",
    )(scalars, s_qk[None], staged, *qkv_arrays, *row_blocks)

    sinks = jnp.pad(sink_kv[0], ((0, 0), (0, 128 - SINK), (0, 0)))
    attended = [
        pl.pallas_call(
            functools.partial(attention_kernel, own_rows),
            grid=(1,),
            out_shape=jax.ShapeDtypeStruct((new_count, lanes), jnp.bfloat16),
            in_specs=[
                SMEM,
                pl.BlockSpec((new_count, lanes), lambda _, part=part: (0, part)),
                pl.BlockSpec((2, cycle_size, lanes), lambda _, part=part: (0, 0, part)),
                pl.BlockSpec((2, 128, lanes), lambda _, part=part: (0, 0, part)),
            ],
            out_specs=pl.BlockSpec((new_count, lanes), lambda _: (0, 0)),
            scratch_shapes=[
                pltpu.VMEM((own_rows, cycle_size), jnp.float32),
                pltpu.VMEM((own_rows, cycle_size), jnp.float32),
            ],
            compiler_params=PARAMS,
        )(scalars, queries, new_cycle, sinks)
        for part in range(parts)
    ]

    groups = {"a": slice(2 * own_rows, new_count), "b": slice(0, 2 * own_rows)}

    def halves(rows):
        size = (rows.stop - rows.start) // 2
        return (jax.ShapeDtypeStruct((size, model_width), jnp.bfloat16),) * 2

    def mix(group):
        rows = groups[group]
        return pl.pallas_call(
            functools.partial(mix_kernel, out_spots, len(out_arrays), parts, own_rows, rows),
            out_shape=halves(rows),
            in_specs=[SMEM] + [VMEM] * (parts + len(out_arrays)),
            out_specs=(VMEM, VMEM),
            scratch_shapes=[pltpu.VMEM((model_width, local_cols), jnp.bfloat16)],
            compiler_params=PARAMS,
        )(scalars, *attended, *out_arrays)

    far = here.core_sum(mix("a"))
    near = here.core_sum(mix("b"))
    sums = [part.astype(jnp.bfloat16) for part in [near, *jnp.split(far, nx - 1)]]
    totals = [part.astype(jnp.float32) for part in sums]
    for step in range(1, nx):
        for d in reversed(range(nx)):
            moved = here.to_x(sums[d], step)
            totals[(d + step) % nx] += moved.astype(jnp.float32)
    after = []
    after_blocks = []
    for d in range(nx):
        residual = row_blocks[2 * d].astype(jnp.float32)
        stepped = residual + alpha_attn * (rms_unit(totals[d]) - residual)
        after.append(rms_unit(stepped).astype(jnp.bfloat16))
        after_blocks += [after[d], here.swap_core(after[d])]

    tile = 256 if units % 256 == 0 else 128
    piece_rows = gated_arrays[0].shape[1]
    active = pl.pallas_call(
        functools.partial(units_kernel, gated_spots, len(gated_arrays), blocks),
        grid=(units // tile,),
        out_shape=jax.ShapeDtypeStruct((new_count, units), jnp.bfloat16),
        in_specs=[SMEM]
        + [pl.BlockSpec((1, tile), lambda n: (0, n))] * 2
        + [pl.BlockSpec((2, piece_rows, tile), lambda n: (0, 0, n))] * len(gated_arrays)
        + [pl.BlockSpec((own_rows, model_width), lambda n: (0, 0))] * blocks,
        out_specs=pl.BlockSpec((new_count, tile), lambda n: (0, n)),
        scratch_shapes=[pltpu.VMEM((2, model_width, tile), jnp.bfloat16)],
        compiler_params=PARAMS,
        name="units",
    )(scalars, s_up[None], s_gate[None], *gated_arrays, *after_blocks)

    down_arrays = [*first_arrays, *second_arrays]

    def lower(group):
        rows = groups[group]
        counts = (len(first_arrays), len(second_arrays))
        return pl.pallas_call(
            functools.partial(lower_kernel, (first_spots, second_spots), counts, own_rows, rows),
            out_shape=halves(rows),
            in_specs=[SMEM] + [VMEM] * (1 + len(down_arrays)),
            out_specs=(VMEM, VMEM),
            scratch_shapes=[pltpu.VMEM((model_width, units), jnp.bfloat16)],
            compiler_params=PARAMS,
        )(scalars, active, *down_arrays)

    far = jnp.split(here.core_sum(lower("a")), nx - 1)
    lowered = here.core_sum(lower("b"))
    for d in range(1, nx):
        moved = here.to_x(far[d - 1].astype(jnp.bfloat16), -d)
        lowered += moved.astype(jnp.float32)
    own_wide = after[0].astype(jnp.float32)
    result = rms_unit(own_wide + alpha_mlp * (rms_unit(lowered) - own_wide)).astype(jnp.bfloat16)
    return (result[None], new_cycle[None])


def solution(mesh):
    axes = (mesh.shape["gx"], mesh.shape["gy"])

    def body(*args):
        return per_device(axes, *args)

    return jax.shard_map(
        body,
        mesh=mesh,
        in_specs=(
            P("gy", "gx", None),
            P("gy"),
            P("gy", None, None, "gx"),
            P("gy", None, None, "gx"),
            P("gy", None, "gx"),
            P("gx"),
            P("gx", "gy"),
            P(),
            P("gy", "gx"),
            P("gy", "gx"),
            P("gx"),
            P("gx"),
            P("gx", "gy"),
            P(),
        ),
        out_specs=(P("gy", "gx", None), P("gy", None, None, "gx")),
        check_vma=False,
    )
```

```python
import functools
import math

import jax
import jax.numpy as jnp
from jax import lax
from jax.experimental import pallas as pl
from jax.experimental.pallas import tpu as pltpu
from jax.sharding import PartitionSpec as P


HD = 64
SINK = 4
WINDOW = 4096
SHORT_KEYS = 768
CHUNK = 512
NEG = -1e30
FIXED = 4
VMEM = pl.BlockSpec(memory_space=pltpu.VMEM)
SMEM = pl.BlockSpec(memory_space=pltpu.SMEM)
ANY = pl.BlockSpec(memory_space=pl.ANY)
PARAMS = pltpu.CompilerParams(vmem_limit_bytes=67043328)


class Layout:
    def __init__(self, gx, gy):
        self.plain = (gx, gy) != (4, 8)
        self.nx = gx // 2
        self.ny = self.nx
        self.nz = gy // self.ny
        mine_x, mine_y = lax.axis_index("gx"), lax.axis_index("gy")
        self.x, self.c = mine_x // 2, mine_x % 2
        self.z, self.y = mine_y // self.ny, mine_y % self.ny

    def from_z(self, value):
        pairs = [
            (z * self.ny + y, (z - 1) % self.nz * self.ny + y)
            for z in range(self.nz)
            for y in range(self.ny)
        ]
        return lax.ppermute(value, "gy", pairs)

    def from_y(self, value):
        pairs = [
            (z * self.ny + y, z * self.ny + (y - 1) % self.ny)
            for z in range(self.nz)
            for y in range(self.ny)
        ]
        return lax.ppermute(value, "gy", pairs)

    def to_x(self, value, step):
        pairs = [
            (x * 2 + c, (x + step) % self.nx * 2 + c) for x in range(self.nx) for c in range(2)
        ]
        return lax.ppermute(value, "gx", pairs)

    def swap_core(self, value):
        pairs = [(x * 2 + c, x * 2 + 1 - c) for x in range(self.nx) for c in range(2)]
        return lax.ppermute(value, "gx", pairs)

    def blocks(self):
        if self.plain:
            return [jnp.int32(0)]
        return [
            (self.z + k) % self.nz * self.ny + (self.y + j) % self.ny
            for k in range(self.nz)
            for j in range(self.ny)
        ]

    def gather(self, shard):
        if self.plain:
            return [(lax.all_gather(shard, "gy", axis=shard.ndim - 2, tiled=True), ())]
        pieces = []
        held = shard
        for k in range(self.nz):
            if k:
                held = self.from_z(held)
            side = held
            for j in range(self.ny):
                if j:
                    side = self.from_y(side)
                pieces.append((side, ()))
        return pieces

    def gather_y_first(self, shard):
        if self.plain:
            return self.gather(shard)
        held = [shard]
        for _ in range(1, self.ny):
            held.append(self.from_y(held[-1]))
        held = jnp.stack(held)
        pieces = []
        for k in range(self.nz):
            if k:
                held = self.from_z(held)
            pieces += [(held, (j,)) for j in range(self.ny)]
        return pieces

    def core_sum(self, halves):
        kept, sent = halves
        return kept.astype(jnp.float32) + self.swap_core(sent).astype(jnp.float32)


def pieces_of(pieces):
    arrays, spots = [], []
    for array, index in pieces:
        known = [n for n, other in enumerate(arrays) if other is array]
        if not known:
            arrays.append(array)
        spots.append((known[0] if known else len(arrays) - 1, index))
    return arrays, tuple(spots)


def place(scalars, refs, spots, held, plane=(), lane=0):
    for n, (number, index) in enumerate(spots):
        value = refs[number][index + plane]
        rows, lanes = value.shape
        at = pl.multiple_of(scalars[FIXED + n] * rows, 16)
        held[pl.ds(at, rows), lane : lane + lanes] = value


def split_rows(value, kept_ref, sent_ref, own_rows):
    for d in range(value.shape[0] // (2 * own_rows)):
        at = slice(d * own_rows, (d + 1) * own_rows)
        kept_ref[at, :] = value[2 * d * own_rows : (2 * d + 1) * own_rows]
        sent_ref[at, :] = value[(2 * d + 1) * own_rows : (2 * d + 2) * own_rows]


def rms_unit(values):
    mean = jnp.sum(values * values, axis=-1, keepdims=True) * (1.0 / values.shape[-1])
    return values * lax.rsqrt(mean + 1e-06)


def step_towards(base, change, alpha):
    return rms_unit(base + alpha * (rms_unit(change) - base)).astype(jnp.bfloat16)


def stage_kernel(source, *rest):
    target = rest[-1]
    target[...] = source[...]


def norm_kernel(base_ref, alpha_ref, *refs):
    terms, out_ref = refs[:-1], refs[-1]
    change = terms[0][...].astype(jnp.float32)
    for term in terms[1:]:
        change += term[...].astype(jnp.float32)
    out_ref[...] = step_towards(base_ref[...].astype(jnp.float32), change, alpha_ref[...])


def qkv_kernel(spots, count, blocks, own_rows, scalars, scale_ref, cycle_in, *rest):
    pieces, row_refs = rest[:count], rest[count : count + blocks]
    query_ref, cycle_ref, window, fresh, held, sems = rest[count + blocks :]
    del cycle_in
    length, x, c, nx = scalars[0], scalars[1], scalars[2], scalars[3]
    new_count, local_cols = query_ref.shape
    cycle_size = cycle_ref.shape[1]
    span = window.shape[1]
    start = lax.rem(length - SINK, cycle_size)
    base = jnp.minimum(start // 16 * 16, cycle_size - span)
    base = pl.multiple_of(base, 16)
    loads = [
        pltpu.make_async_copy(cycle_ref.at[i, pl.ds(base, span), :], window.at[i], sems.at[i])
        for i in range(2)
    ]
    for load in loads:
        load.start()
    rows = jnp.concatenate([ref[...] for ref in row_refs], axis=0)
    lane_head = lax.broadcasted_iota(jnp.int32, (1, local_cols), 1) // HD

    def unit(values):
        squares = values * values
        total = jnp.zeros_like(values)
        for head in range(local_cols // HD):
            picked = lane_head == head
            part = jnp.sum(jnp.where(picked, squares, 0.0), axis=-1, keepdims=True)
            total = jnp.where(picked, part, total)
        return values * lax.rsqrt(total + 1e-06) * scale_ref[...]

    def project(which):
        place(scalars, pieces, spots, held.at[which], (which,))
        return jnp.dot(rows, held[which], preferred_element_type=jnp.float32)

    queries = unit(project(0)).astype(jnp.bfloat16)
    query_ref[...] = (queries.astype(jnp.float32) * math.sqrt(HD)).astype(jnp.bfloat16)
    fresh[0] = unit(project(1)).astype(jnp.bfloat16)
    fresh[1] = project(2).astype(jnp.bfloat16)
    row = lax.broadcasted_iota(jnp.int32, (1, new_count), 1)
    block, inside = row // own_rows, row % own_rows
    from_x = lax.rem(x - block // 2 + nx, nx)
    from_c = jnp.where(block % 2 == 1, 1 - c, c)
    token = (from_x * 2 + from_c) * own_rows + inside
    target = token + (start - base)
    slot = lax.broadcasted_iota(jnp.int32, (span, 1), 0)
    pick = (slot == target).astype(jnp.float32).astype(jnp.bfloat16)
    offset = slot - (start - base)
    replaced = (offset >= 0) & (offset < new_count)
    stores = []
    for i in range(2):
        loads[i].wait()
        moved = jnp.dot(pick, fresh[i], preferred_element_type=jnp.float32)
        window[i] = jnp.where(replaced, moved, window[i].astype(jnp.float32)).astype(jnp.bfloat16)
        store = pltpu.make_async_copy(
            window.at[i], cycle_ref.at[i, pl.ds(base, span), :], sems.at[i]
        )
        store.start()
        stores.append(store)
    for store in stores:
        store.wait()


def attention_kernel(own_rows, scalars, query_ref, cycle_ref, sink_ref, out_ref, scores, bias):
    length, x, c, nx = scalars[0], scalars[1], scalars[2], scalars[3]
    new_count, lanes = query_ref.shape
    cycle_size = cycle_ref.shape[1]
    lane_head = lax.broadcasted_iota(jnp.int32, (1, lanes), 1) // HD
    sink_lane = lax.broadcasted_iota(jnp.int32, (1, sink_ref.shape[1]), 1)
    sink_bias = jnp.where(sink_lane < SINK, 0.0, NEG)
    contract = (((1,), (1,)), ((), ()))

    def run(keys):
        sizes = [min(CHUNK, keys - at) for at in range(0, keys, CHUNK)]
        starts = [CHUNK * n for n in range(len(sizes))]

        def tile(i, _):
            from_x = lax.rem(x - i // 2 + nx, nx)
            from_c = jnp.where(i % 2 == 1, 1 - c, c)
            first = (from_x * 2 + from_c) * own_rows
            at = pl.multiple_of(i * own_rows, own_rows)
            queries = query_ref[pl.ds(at, own_rows), :]
            moment = first + lax.broadcasted_iota(jnp.int32, (own_rows, 1), 0)
            for begin, size in zip(starts, sizes):
                slot = begin + lax.broadcasted_iota(jnp.int32, (1, size), 1)
                lagging = length + new_count - 1 - SINK - slot
                turn = cycle_size * (jnp.maximum(lagging, 0) // cycle_size)
                ahead = jnp.where(lagging >= 0, SINK + slot + turn - length, 1 << 20)
                lag = moment - ahead
                seen = (lag >= 0) & (lag < WINDOW)
                bias[:, begin : begin + size] = jnp.where(seen, 0.0, NEG)
            result = jnp.zeros((own_rows, lanes), jnp.float32)
            for head in range(lanes // HD):
                mine = lane_head == head
                picked = jnp.where(mine, queries.astype(jnp.float32), 0.0).astype(jnp.bfloat16)
                sink_scores = (
                    lax.dot_general(
                        picked, sink_ref[0], contract, preferred_element_type=jnp.float32
                    )
                    + sink_bias
                )
                highest = jnp.max(sink_scores, axis=-1, keepdims=True)
                for begin, size in zip(starts, sizes):
                    part = lax.dot_general(
                        picked,
                        cycle_ref[0, begin : begin + size, :],
                        contract,
                        preferred_element_type=jnp.float32,
                    )
                    part = part + bias[:, begin : begin + size]
                    scores[:, begin : begin + size] = part
                    highest = jnp.maximum(highest, jnp.max(part, axis=-1, keepdims=True))
                weights = jnp.exp(sink_scores - highest)
                total = jnp.sum(weights, axis=-1, keepdims=True)
                summed = jnp.dot(
                    weights.astype(jnp.bfloat16), sink_ref[1], preferred_element_type=jnp.float32
                )
                for begin, size in zip(starts, sizes):
                    weights = jnp.exp(scores[:, begin : begin + size] - highest)
                    total += jnp.sum(weights, axis=-1, keepdims=True)
                    summed += jnp.dot(
                        weights.astype(jnp.bfloat16),
                        cycle_ref[1, begin : begin + size, :],
                        preferred_element_type=jnp.float32,
                    )
                result = jnp.where(mine, summed / total, result)
            out_ref[pl.ds(at, own_rows), :] = result.astype(jnp.bfloat16)
            return 0

        lax.fori_loop(0, new_count // own_rows, tile, 0)

    few = length + new_count - SINK <= SHORT_KEYS

    @pl.when(few)
    def _():
        run(SHORT_KEYS)

    @pl.when(jnp.logical_not(few))
    def _():
        run(cycle_size)


def mix_kernel(spots, count, parts, own_rows, rows, scalars, *refs):
    attended, pieces = refs[:parts], refs[parts : parts + count]
    kept_ref, sent_ref, held = refs[parts + count :]
    place(scalars, pieces, spots, held)
    wide = jnp.concatenate([ref[rows, :] for ref in attended], axis=1)
    mixed = lax.dot_general(
        wide, held[...], (((1,), (1,)), ((), ())), preferred_element_type=jnp.float32
    ).astype(jnp.bfloat16)
    split_rows(mixed, kept_ref, sent_ref, own_rows)


def units_kernel(spots, count, blocks, scalars, up_scale, gate_scale, *refs):
    pieces, row_refs = refs[:count], refs[count : count + blocks]
    out_ref, held = refs[count + blocks :]
    rows = jnp.concatenate([ref[...] for ref in row_refs], axis=0)
    for plane in range(2):
        place(scalars, pieces, spots, held.at[plane], (plane,))
    up = jnp.dot(rows, held[0], preferred_element_type=jnp.float32) * up_scale[...]
    gate = jnp.dot(rows, held[1], preferred_element_type=jnp.float32) * gate_scale[...]
    out_ref[...] = (up * (gate / (1.0 + jnp.exp(-gate)))).astype(jnp.bfloat16)


def lower_kernel(spots, counts, own_rows, rows, scalars, active_ref, *refs):
    kept_ref, sent_ref, held = refs[sum(counts) :]
    lane = 0
    for n, count in enumerate(counts):
        pieces = refs[sum(counts[:n]) : sum(counts[: n + 1])]
        place(scalars, pieces, spots[n], held, lane=lane)
        lane += pieces[0].shape[-1]
    lowered = lax.dot_general(
        active_ref[rows, :], held[...], (((1,), (1,)), ((), ())), preferred_element_type=jnp.float32
    ).astype(jnp.bfloat16)
    split_rows(lowered, kept_ref, sent_ref, own_rows)


def per_device(
    axes,
    hidden,
    lengths,
    sink_kv,
    kv_cycle,
    w_qkv,
    s_qk,
    w_out,
    alpha_attn,
    w_up,
    w_gate,
    s_up,
    s_gate,
    w_down,
    alpha_mlp,
):
    here = Layout(*axes)
    _, own_rows, model_width = hidden.shape
    nx, blocks = here.nx, axes[0]
    new_count = own_rows * blocks
    local_cols = s_qk.shape[0]
    cycle_size = kv_cycle.shape[2]
    units = s_up.shape[0]
    lanes = min(128, local_cols)
    parts = local_cols // lanes
    span = min(new_count + 16, cycle_size)
    chunk = cycle_size // 9

    row_blocks = []
    for d in range(nx):
        block = here.to_x(hidden[0], d) if d else hidden[0]
        row_blocks += [block, here.swap_core(block)]

    qkv_arrays, qkv_spots = pieces_of(here.gather(w_qkv.transpose(1, 0, 2)))
    out_arrays, out_spots = pieces_of(here.gather_y_first(w_out.T))
    gated_arrays, gated_spots = pieces_of(here.gather(jnp.stack([w_up, w_gate])))
    lower_t = w_down.T
    half = units // 2
    first_arrays, first_spots = pieces_of(here.gather_y_first(lower_t[:, :half]))
    second_arrays, second_spots = pieces_of(here.gather(lower_t[:, half:]))

    scalars = jnp.stack([lengths[0], here.x, here.c, jnp.int32(nx), *here.blocks()])
    sinks = jnp.pad(sink_kv[0], ((0, 0), (0, 128 - SINK), (0, 0)))
    vectors = [s_qk[None], s_up[None], s_gate[None], alpha_attn[None], alpha_mlp[None]]
    early = [scalars, sinks, *vectors]
    scale_qk, scale_up, scale_gate, alpha_attn, alpha_mlp = vectors
    staged = pl.pallas_call(
        stage_kernel,
        grid=(9,),
        out_shape=jax.ShapeDtypeStruct(kv_cycle.shape[1:], jnp.bfloat16),
        in_specs=[pl.BlockSpec((2, chunk, local_cols), lambda n: (0, n, 0))]
        + [ANY] * len(early),
        out_specs=pl.BlockSpec((2, chunk, local_cols), lambda n: (0, n, 0)),
        compiler_params=PARAMS,
        name="stage",
    )(kv_cycle[0], *early)
    queries, new_cycle = pl.pallas_call(
        functools.partial(qkv_kernel, qkv_spots, len(qkv_arrays), blocks, own_rows),
        out_shape=(
            jax.ShapeDtypeStruct((new_count, local_cols), jnp.bfloat16),
            jax.ShapeDtypeStruct(kv_cycle.shape[1:], jnp.bfloat16),
        ),
        in_specs=[SMEM, VMEM, ANY] + [VMEM] * (len(qkv_arrays) + blocks),
        out_specs=(VMEM, ANY),
        scratch_shapes=[
            pltpu.VMEM((2, span, local_cols), jnp.bfloat16),
            pltpu.VMEM((2, new_count, local_cols), jnp.bfloat16),
            pltpu.VMEM((3, model_width, local_cols), jnp.bfloat16),
            pltpu.SemaphoreType.DMA((2,)),
        ],
        input_output_aliases={2: 1},
        compiler_params=PARAMS,
        name="qkv",
    )(scalars, scale_qk, staged, *qkv_arrays, *row_blocks)

    attended = [
        pl.pallas_call(
            functools.partial(attention_kernel, own_rows),
            grid=(1,),
            out_shape=jax.ShapeDtypeStruct((new_count, lanes), jnp.bfloat16),
            in_specs=[
                SMEM,
                pl.BlockSpec((new_count, lanes), lambda _, part=part: (0, part)),
                pl.BlockSpec((2, cycle_size, lanes), lambda _, part=part: (0, 0, part)),
                pl.BlockSpec((2, 128, lanes), lambda _, part=part: (0, 0, part)),
            ],
            out_specs=pl.BlockSpec((new_count, lanes), lambda _: (0, 0)),
            scratch_shapes=[
                pltpu.VMEM((own_rows, cycle_size), jnp.float32),
                pltpu.VMEM((own_rows, cycle_size), jnp.float32),
            ],
            compiler_params=PARAMS,
        )(scalars, queries, new_cycle, sinks)
        for part in range(parts)
    ]

    groups = {"a": slice(2 * own_rows, new_count), "b": slice(0, 2 * own_rows)}

    def halves(rows):
        size = (rows.stop - rows.start) // 2
        return (jax.ShapeDtypeStruct((size, model_width), jnp.bfloat16),) * 2

    def mix(group):
        rows = groups[group]
        return pl.pallas_call(
            functools.partial(mix_kernel, out_spots, len(out_arrays), parts, own_rows, rows),
            out_shape=halves(rows),
            in_specs=[SMEM] + [VMEM] * (parts + len(out_arrays)),
            out_specs=(VMEM, VMEM),
            scratch_shapes=[pltpu.VMEM((model_width, local_cols), jnp.bfloat16)],
            compiler_params=PARAMS,
        )(scalars, *attended, *out_arrays)

    far = here.core_sum(mix("a"))
    near = here.core_sum(mix("b"))
    sums = [part.astype(jnp.bfloat16) for part in [near, *jnp.split(far, nx - 1)]]
    totals = [[part] for part in sums]
    for step in range(1, nx):
        for d in reversed(range(nx)):
            moved = here.to_x(sums[d], step)
            totals[(d + step) % nx].append(moved)

    def norm(base, alpha, terms):
        return pl.pallas_call(
            norm_kernel,
            out_shape=jax.ShapeDtypeStruct(base.shape, jnp.bfloat16),
            in_specs=[VMEM] * (2 + len(terms)),
            out_specs=VMEM,
            compiler_params=PARAMS,
        )(base, alpha, *terms)

    after = []
    after_blocks = []
    for d in range(nx):
        after.append(norm(row_blocks[2 * d], alpha_attn, totals[d]))
        after_blocks += [after[d], here.swap_core(after[d])]

    tile = 256 if units % 256 == 0 else 128
    piece_rows = gated_arrays[0].shape[1]
    active = pl.pallas_call(
        functools.partial(units_kernel, gated_spots, len(gated_arrays), blocks),
        grid=(units // tile,),
        out_shape=jax.ShapeDtypeStruct((new_count, units), jnp.bfloat16),
        in_specs=[SMEM]
        + [pl.BlockSpec((1, tile), lambda n: (0, n))] * 2
        + [pl.BlockSpec((2, piece_rows, tile), lambda n: (0, 0, n))] * len(gated_arrays)
        + [pl.BlockSpec((own_rows, model_width), lambda n: (0, 0))] * blocks,
        out_specs=pl.BlockSpec((new_count, tile), lambda n: (0, n)),
        scratch_shapes=[pltpu.VMEM((2, model_width, tile), jnp.bfloat16)],
        compiler_params=PARAMS,
        name="units",
    )(scalars, scale_up, scale_gate, *gated_arrays, *after_blocks)

    down_arrays = [*first_arrays, *second_arrays]

    def lower(group):
        rows = groups[group]
        counts = (len(first_arrays), len(second_arrays))
        return pl.pallas_call(
            functools.partial(lower_kernel, (first_spots, second_spots), counts, own_rows, rows),
            out_shape=halves(rows),
            in_specs=[SMEM] + [VMEM] * (1 + len(down_arrays)),
            out_specs=(VMEM, VMEM),
            scratch_shapes=[pltpu.VMEM((model_width, units), jnp.bfloat16)],
            compiler_params=PARAMS,
        )(scalars, active, *down_arrays)

    far = jnp.split(here.core_sum(lower("a")).astype(jnp.bfloat16), nx - 1)
    kept, sent = lower("b")
    terms = [kept, here.swap_core(sent)]
    terms += [here.to_x(far[d - 1], -d) for d in range(1, nx)]
    result = norm(after[0], alpha_mlp, terms)
    return (result[None], new_cycle[None])


def solution(mesh):
    axes = (mesh.shape["gx"], mesh.shape["gy"])

    def body(*args):
        return per_device(axes, *args)

    return jax.shard_map(
        body,
        mesh=mesh,
        in_specs=(
            P("gy", "gx", None),
            P("gy"),
            P("gy", None, None, "gx"),
            P("gy", None, None, "gx"),
            P("gy", None, "gx"),
            P("gx"),
            P("gx", "gy"),
            P(),
            P("gy", "gx"),
            P("gy", "gx"),
            P("gx"),
            P("gx"),
            P("gx", "gy"),
            P(),
        ),
        out_specs=(P("gy", "gx", None), P("gy", None, None, "gx")),
        check_vma=False,
    )
```

```python
import functools
import math

import jax
import jax.numpy as jnp
from jax import lax
from jax.experimental import pallas as pl
from jax.experimental.pallas import tpu as pltpu
from jax.sharding import PartitionSpec as P


HD = 64
SINK = 4
WINDOW = 4096
SHORT_KEYS = 768
CHUNK = 512
NEG = -1e30
FIXED = 4
VMEM = pl.BlockSpec(memory_space=pltpu.VMEM)
SMEM = pl.BlockSpec(memory_space=pltpu.SMEM)
ANY = pl.BlockSpec(memory_space=pl.ANY)
PARAMS = pltpu.CompilerParams(vmem_limit_bytes=67043328)
LIGHT = pltpu.CompilerParams(vmem_limit_bytes=24 << 20)


class Layout:
    def __init__(self, gx, gy):
        self.plain = (gx, gy) != (4, 8)
        self.nx = gx // 2
        self.ny = self.nx
        self.nz = gy // self.ny
        mine_x, mine_y = lax.axis_index("gx"), lax.axis_index("gy")
        self.x, self.c = mine_x // 2, mine_x % 2
        self.z, self.y = mine_y // self.ny, mine_y % self.ny

    def from_z(self, value):
        pairs = [
            (z * self.ny + y, (z - 1) % self.nz * self.ny + y)
            for z in range(self.nz)
            for y in range(self.ny)
        ]
        return lax.ppermute(value, "gy", pairs)

    def from_y(self, value):
        pairs = [
            (z * self.ny + y, z * self.ny + (y - 1) % self.ny)
            for z in range(self.nz)
            for y in range(self.ny)
        ]
        return lax.ppermute(value, "gy", pairs)

    def to_x(self, value, step):
        pairs = [
            (x * 2 + c, (x + step) % self.nx * 2 + c) for x in range(self.nx) for c in range(2)
        ]
        return lax.ppermute(value, "gx", pairs)

    def swap_core(self, value):
        pairs = [(x * 2 + c, x * 2 + 1 - c) for x in range(self.nx) for c in range(2)]
        return lax.ppermute(value, "gx", pairs)

    def blocks(self):
        if self.plain:
            return [jnp.int32(0)]
        return [
            (self.z + k) % self.nz * self.ny + (self.y + j) % self.ny
            for k in range(self.nz)
            for j in range(self.ny)
        ]

    def gather(self, shard):
        if self.plain:
            return [(lax.all_gather(shard, "gy", axis=shard.ndim - 2, tiled=True), ())]
        pieces = []
        held = shard
        for k in range(self.nz):
            if k:
                held = self.from_z(held)
            side = held
            for j in range(self.ny):
                if j:
                    side = self.from_y(side)
                pieces.append((side, ()))
        return pieces

    def gather_y_first(self, shard):
        if self.plain:
            return self.gather(shard)
        held = [shard]
        for _ in range(1, self.ny):
            held.append(self.from_y(held[-1]))
        held = jnp.stack(held)
        pieces = []
        for k in range(self.nz):
            if k:
                held = self.from_z(held)
            pieces += [(held, (j,)) for j in range(self.ny)]
        return pieces

    def core_sum(self, halves):
        kept, sent = halves
        return kept.astype(jnp.float32) + self.swap_core(sent).astype(jnp.float32)


def pieces_of(pieces):
    arrays, spots = [], []
    for array, index in pieces:
        known = [n for n, other in enumerate(arrays) if other is array]
        if not known:
            arrays.append(array)
        spots.append((known[0] if known else len(arrays) - 1, index))
    return arrays, tuple(spots)


def place(scalars, refs, spots, held, plane=(), lane=0):
    for n, (number, index) in enumerate(spots):
        value = refs[number][index + plane]
        rows, lanes = value.shape
        at = pl.multiple_of(scalars[FIXED + n] * rows, 16)
        held[pl.ds(at, rows), lane : lane + lanes] = value


def split_rows(value, kept_ref, sent_ref, own_rows):
    for d in range(value.shape[0] // (2 * own_rows)):
        at = slice(d * own_rows, (d + 1) * own_rows)
        kept_ref[at, :] = value[2 * d * own_rows : (2 * d + 1) * own_rows]
        sent_ref[at, :] = value[(2 * d + 1) * own_rows : (2 * d + 2) * own_rows]


def rms_unit(values):
    mean = jnp.sum(values * values, axis=-1, keepdims=True) * (1.0 / values.shape[-1])
    return values * lax.rsqrt(mean + 1e-06)


def step_towards(base, change, alpha):
    return rms_unit(base + alpha * (rms_unit(change) - base)).astype(jnp.bfloat16)


def stage_kernel(source, *rest):
    target = rest[-1]
    target[...] = source[...]


def norm_kernel(row, base_ref, alpha_ref, *refs):
    terms, out_ref = refs[:-1], refs[-1]
    change = terms[0][...].astype(jnp.float32)
    for term in terms[1:]:
        change += term[...].astype(jnp.float32)
    out_ref[...] = step_towards(base_ref[...].astype(jnp.float32), change, alpha_ref[row : row + 1, :])


def qkv_kernel(spots, count, blocks, own_rows, scalars, scale_ref, cycle_in, *rest):
    pieces, row_refs = rest[:count], rest[count : count + blocks]
    query_ref, cycle_ref, window, fresh, held, sems = rest[count + blocks :]
    del cycle_in
    length, x, c, nx = scalars[0], scalars[1], scalars[2], scalars[3]
    new_count, local_cols = query_ref.shape
    cycle_size = cycle_ref.shape[1]
    span = window.shape[1]
    start = lax.rem(length - SINK, cycle_size)
    base = jnp.minimum(start // 16 * 16, cycle_size - span)
    base = pl.multiple_of(base, 16)
    loads = [
        pltpu.make_async_copy(cycle_ref.at[i, pl.ds(base, span), :], window.at[i], sems.at[i])
        for i in range(2)
    ]
    for load in loads:
        load.start()
    rows = jnp.concatenate([ref[...] for ref in row_refs], axis=0)
    lane_head = lax.broadcasted_iota(jnp.int32, (1, local_cols), 1) // HD

    def unit(values):
        squares = values * values
        total = jnp.zeros_like(values)
        for head in range(local_cols // HD):
            picked = lane_head == head
            part = jnp.sum(jnp.where(picked, squares, 0.0), axis=-1, keepdims=True)
            total = jnp.where(picked, part, total)
        return values * lax.rsqrt(total + 1e-06) * scale_ref[...]

    def project(which):
        place(scalars, pieces, spots, held.at[which], (which,))
        return jnp.dot(rows, held[which], preferred_element_type=jnp.float32)

    queries = unit(project(0)).astype(jnp.bfloat16)
    query_ref[...] = (queries.astype(jnp.float32) * math.sqrt(HD)).astype(jnp.bfloat16)
    fresh[0] = unit(project(1)).astype(jnp.bfloat16)
    fresh[1] = project(2).astype(jnp.bfloat16)
    row = lax.broadcasted_iota(jnp.int32, (1, new_count), 1)
    block, inside = row // own_rows, row % own_rows
    from_x = lax.rem(x - block // 2 + nx, nx)
    from_c = jnp.where(block % 2 == 1, 1 - c, c)
    token = (from_x * 2 + from_c) * own_rows + inside
    target = token + (start - base)
    slot = lax.broadcasted_iota(jnp.int32, (span, 1), 0)
    pick = (slot == target).astype(jnp.float32).astype(jnp.bfloat16)
    offset = slot - (start - base)
    replaced = (offset >= 0) & (offset < new_count)
    stores = []
    for i in range(2):
        loads[i].wait()
        moved = jnp.dot(pick, fresh[i], preferred_element_type=jnp.float32)
        window[i] = jnp.where(replaced, moved, window[i].astype(jnp.float32)).astype(jnp.bfloat16)
        store = pltpu.make_async_copy(
            window.at[i], cycle_ref.at[i, pl.ds(base, span), :], sems.at[i]
        )
        store.start()
        stores.append(store)
    for store in stores:
        store.wait()


def attention_kernel(own_rows, scalars, query_ref, cycle_ref, sink_ref, out_ref, pair, bias):
    length, x, c, nx = scalars[0], scalars[1], scalars[2], scalars[3]
    new_count, lanes = query_ref.shape
    cycle_size = cycle_ref.shape[1]
    lane_head = lax.broadcasted_iota(jnp.int32, (1, lanes), 1) // HD
    sink_lane = lax.broadcasted_iota(jnp.int32, (1, sink_ref.shape[1]), 1)
    sink_bias = jnp.where(sink_lane < SINK, 0.0, NEG)
    contract = (((1,), (1,)), ((), ()))
    scores = pair.at[0]

    def run(keys):
        sizes = [min(CHUNK, keys - at) for at in range(0, keys, CHUNK)]
        starts = [CHUNK * n for n in range(len(sizes))]

        def tile(i, _):
            from_x = lax.rem(x - i // 2 + nx, nx)
            from_c = jnp.where(i % 2 == 1, 1 - c, c)
            first = (from_x * 2 + from_c) * own_rows
            at = pl.multiple_of(i * own_rows, own_rows)
            queries = query_ref[pl.ds(at, own_rows), :]
            moment = first + lax.broadcasted_iota(jnp.int32, (own_rows, 1), 0)
            for begin, size in zip(starts, sizes):
                slot = begin + lax.broadcasted_iota(jnp.int32, (1, size), 1)
                lagging = length + new_count - 1 - SINK - slot
                turn = cycle_size * (jnp.maximum(lagging, 0) // cycle_size)
                ahead = jnp.where(lagging >= 0, SINK + slot + turn - length, 1 << 20)
                lag = moment - ahead
                seen = (lag >= 0) & (lag < WINDOW)
                bias[0, :, begin : begin + size] = jnp.where(seen, 0.0, NEG)
            result = jnp.zeros((own_rows, lanes), jnp.float32)
            for head in range(lanes // HD):
                mine = lane_head == head
                picked = jnp.where(mine, queries.astype(jnp.float32), 0.0).astype(jnp.bfloat16)
                sink_scores = (
                    lax.dot_general(
                        picked, sink_ref[0], contract, preferred_element_type=jnp.float32
                    )
                    + sink_bias
                )
                highest = jnp.max(sink_scores, axis=-1, keepdims=True)
                for begin, size in zip(starts, sizes):
                    part = lax.dot_general(
                        picked,
                        cycle_ref[0, begin : begin + size, :],
                        contract,
                        preferred_element_type=jnp.float32,
                    )
                    part = part + bias[0, :, begin : begin + size]
                    scores[:, begin : begin + size] = part
                    highest = jnp.maximum(highest, jnp.max(part, axis=-1, keepdims=True))
                weights = jnp.exp(sink_scores - highest)
                total = jnp.sum(weights, axis=-1, keepdims=True)
                summed = jnp.dot(
                    weights.astype(jnp.bfloat16), sink_ref[1], preferred_element_type=jnp.float32
                )
                for begin, size in zip(starts, sizes):
                    weights = jnp.exp(scores[:, begin : begin + size] - highest)
                    total += jnp.sum(weights, axis=-1, keepdims=True)
                    summed += jnp.dot(
                        weights.astype(jnp.bfloat16),
                        cycle_ref[1, begin : begin + size, :],
                        preferred_element_type=jnp.float32,
                    )
                result = jnp.where(mine, summed / total, result)
            out_ref[pl.ds(at, own_rows), :] = result.astype(jnp.bfloat16)
            return 0

        lax.fori_loop(0, new_count // own_rows, tile, 0)

    def run_full():
        start = lax.rem(length - SINK, cycle_size)
        chunks = cycle_size // CHUNK
        masked = min((2 * new_count + CHUNK - 1) // CHUNK + 1, chunks)
        firsts = [
            pl.multiple_of(lax.rem(start // CHUNK + n, chunks) * CHUNK, CHUNK) for n in range(chunks)
        ]
        steps = [(i, head) for i in range(new_count // own_rows) for head in range(lanes // HD)]
        queries, highest, results = {}, {}, {}

        def masks(i):
            from_x = lax.rem(x - i // 2 + nx, nx)
            from_c = 1 - c if i % 2 == 1 else c
            moment = (from_x * 2 + from_c) * own_rows + lax.broadcasted_iota(
                jnp.int32, (own_rows, 1), 0
            )
            for n in range(masked):
                slot = firsts[n] + lax.broadcasted_iota(jnp.int32, (1, CHUNK), 1)
                since = slot - start
                since = jnp.where(since < 0, since + cycle_size, since)
                ahead = jnp.where(since < new_count, since, since - cycle_size)
                lag = moment - ahead
                seen = (lag >= 0) & (lag < WINDOW)
                bias[i % 2, :, n * CHUNK : (n + 1) * CHUNK] = jnp.where(seen, 0.0, NEG)

        def score_sinks(u):
            i, head = steps[u]
            rows = query_ref[i * own_rows : (i + 1) * own_rows, :].astype(jnp.float32)
            queries[u] = jnp.where(lane_head == head, rows, 0.0).astype(jnp.bfloat16)
            sink = (
                lax.dot_general(
                    queries[u], sink_ref[0], contract, preferred_element_type=jnp.float32
                )
                + sink_bias
            )
            highest[u] = [sink]
            return sink

        def score(u, n):
            part = lax.dot_general(
                queries[u],
                cycle_ref[0, pl.ds(firsts[n], CHUNK), :],
                contract,
                preferred_element_type=jnp.float32,
            )
            if n < masked:
                part = part + bias[steps[u][0] % 2, :, n * CHUNK : (n + 1) * CHUNK]
            pair[u % 2, :, n * CHUNK : (n + 1) * CHUNK] = part
            for lane in range(0, CHUNK, 128):
                highest[u].append(part[:, lane : lane + 128])
            while len(highest[u]) > 1:
                highest[u] = [
                    jnp.maximum(a, b) for a, b in zip(highest[u][::2], highest[u][1::2])
                ] + highest[u][len(highest[u]) // 2 * 2 :]

        sinks = {}

        def begin(u):
            if steps[u][1] == 0:
                masks(steps[u][0])
            sinks[u] = score_sinks(u)

        begin(0)
        for n in range(chunks):
            score(0, n)
        for u, (i, head) in enumerate(steps):
            top = jnp.max(highest[u][0], axis=-1, keepdims=True)
            weights = jnp.exp(sinks[u] - top)
            lanes_total = weights
            summed = jnp.dot(
                weights.astype(jnp.bfloat16), sink_ref[1], preferred_element_type=jnp.float32
            )
            if u + 1 < len(steps):
                begin(u + 1)
            for n in range(chunks):
                if u + 1 < len(steps):
                    score(u + 1, n)
                weights = jnp.exp(pair[u % 2, :, n * CHUNK : (n + 1) * CHUNK] - top)
                for lane in range(0, CHUNK, 128):
                    lanes_total = lanes_total + weights[:, lane : lane + 128]
                summed += jnp.dot(
                    weights.astype(jnp.bfloat16),
                    cycle_ref[1, pl.ds(firsts[n], CHUNK), :],
                    preferred_element_type=jnp.float32,
                )
            total = jnp.sum(lanes_total, axis=-1, keepdims=True)
            before = results.get(i, jnp.zeros((own_rows, lanes), jnp.float32))
            results[i] = jnp.where(lane_head == head, summed / total, before)
            if head == lanes // HD - 1:
                out_ref[i * own_rows : (i + 1) * own_rows, :] = results[i].astype(jnp.bfloat16)

    few = length + new_count - SINK <= SHORT_KEYS
    full = length - SINK >= cycle_size

    @pl.when(few)
    def _():
        run(SHORT_KEYS)

    @pl.when(full)
    def _():
        run_full()

    @pl.when(jnp.logical_not(few | full))
    def _():
        run(cycle_size)


def mix_kernel(spots, count, parts, own_rows, scalars, *refs):
    attended, pieces = refs[:parts], refs[parts : parts + count]
    kept_ref, sent_ref, held = refs[parts + count :]
    place(scalars, pieces, spots, held)
    wide = jnp.concatenate([ref[...] for ref in attended], axis=1)
    mixed = lax.dot_general(
        wide, held[...], (((1,), (1,)), ((), ())), preferred_element_type=jnp.float32
    ).astype(jnp.bfloat16)
    split_rows(mixed, kept_ref, sent_ref, own_rows)


def units_kernel(spots, count, blocks, scalars, scale_ref, *refs):
    pieces, row_refs = refs[:count], refs[count : count + blocks]
    out_ref, held = refs[count + blocks :]
    rows = jnp.concatenate([ref[...] for ref in row_refs], axis=0)
    for plane in range(2):
        place(scalars, pieces, spots, held.at[plane], (plane,))
    up = jnp.dot(rows, held[0], preferred_element_type=jnp.float32) * scale_ref[:1, :]
    gate = jnp.dot(rows, held[1], preferred_element_type=jnp.float32) * scale_ref[1:, :]
    out_ref[...] = (up * (gate / (1.0 + jnp.exp(-gate)))).astype(jnp.bfloat16)


def lower_kernel(spots, counts, own_rows, rows, scalars, active_ref, *refs):
    kept_ref, sent_ref, held = refs[sum(counts) :]
    lane = 0
    for n, count in enumerate(counts):
        pieces = refs[sum(counts[:n]) : sum(counts[: n + 1])]
        place(scalars, pieces, spots[n], held, lane=lane)
        lane += pieces[0].shape[-1]
    lowered = lax.dot_general(
        active_ref[rows, :], held[...], (((1,), (1,)), ((), ())), preferred_element_type=jnp.float32
    ).astype(jnp.bfloat16)
    split_rows(lowered, kept_ref, sent_ref, own_rows)


def per_device(
    axes,
    hidden,
    lengths,
    sink_kv,
    kv_cycle,
    w_qkv,
    s_qk,
    w_out,
    alpha_attn,
    w_up,
    w_gate,
    s_up,
    s_gate,
    w_down,
    alpha_mlp,
):
    here = Layout(*axes)
    _, own_rows, model_width = hidden.shape
    nx, blocks = here.nx, axes[0]
    new_count = own_rows * blocks
    local_cols = s_qk.shape[0]
    cycle_size = kv_cycle.shape[2]
    units = s_up.shape[0]
    lanes = min(128, local_cols)
    parts = local_cols // lanes
    span = min(new_count + 16, cycle_size)
    chunk = cycle_size // 9

    row_blocks = []
    for d in range(nx):
        block = here.to_x(hidden[0], d) if d else hidden[0]
        row_blocks += [block, here.swap_core(block)]

    qkv_arrays, qkv_spots = pieces_of(here.gather(w_qkv.transpose(1, 0, 2)))
    out_arrays, out_spots = pieces_of(here.gather_y_first(w_out.T))
    gated_arrays, gated_spots = pieces_of(here.gather(jnp.stack([w_up, w_gate])))
    lower_t = w_down.T
    half = units // 2
    first_arrays, first_spots = pieces_of(here.gather_y_first(lower_t[:, :half]))
    second_arrays, second_spots = pieces_of(here.gather(lower_t[:, half:]))

    scalars = jnp.stack([lengths[0], here.x, here.c, jnp.int32(nx), *here.blocks()])
    sinks = jnp.pad(sink_kv[0], ((0, 0), (0, 128 - SINK), (0, 0)))
    scale_qk, scales = s_qk[None], jnp.stack([s_up, s_gate])
    alphas = jnp.stack([alpha_attn, alpha_mlp])
    early = [scalars, sinks, scale_qk, scales, alphas]
    staged = pl.pallas_call(
        stage_kernel,
        grid=(9,),
        out_shape=jax.ShapeDtypeStruct(kv_cycle.shape[1:], jnp.bfloat16),
        in_specs=[pl.BlockSpec((2, chunk, local_cols), lambda n: (0, n, 0))]
        + [ANY] * len(early),
        out_specs=pl.BlockSpec((2, chunk, local_cols), lambda n: (0, n, 0)),
        compiler_params=PARAMS,
        name="stage",
    )(kv_cycle[0], *early)
    queries, new_cycle = pl.pallas_call(
        functools.partial(qkv_kernel, qkv_spots, len(qkv_arrays), blocks, own_rows),
        out_shape=(
            jax.ShapeDtypeStruct((new_count, local_cols), jnp.bfloat16),
            jax.ShapeDtypeStruct(kv_cycle.shape[1:], jnp.bfloat16),
        ),
        in_specs=[SMEM, VMEM, ANY] + [VMEM] * (len(qkv_arrays) + blocks),
        out_specs=(VMEM, ANY),
        scratch_shapes=[
            pltpu.VMEM((2, span, local_cols), jnp.bfloat16),
            pltpu.VMEM((2, new_count, local_cols), jnp.bfloat16),
            pltpu.VMEM((3, model_width, local_cols), jnp.bfloat16),
            pltpu.SemaphoreType.DMA((2,)),
        ],
        input_output_aliases={2: 1},
        compiler_params=PARAMS,
        name="qkv",
    )(scalars, scale_qk, staged, *qkv_arrays, *row_blocks)

    attended = [
        pl.pallas_call(
            functools.partial(attention_kernel, own_rows),
            grid=(1,),
            out_shape=jax.ShapeDtypeStruct((new_count, lanes), jnp.bfloat16),
            in_specs=[
                SMEM,
                pl.BlockSpec((new_count, lanes), lambda _, part=part: (0, part)),
                pl.BlockSpec((2, cycle_size, lanes), lambda _, part=part: (0, 0, part)),
                pl.BlockSpec((2, 128, lanes), lambda _, part=part: (0, 0, part)),
            ],
            out_specs=pl.BlockSpec((new_count, lanes), lambda _: (0, 0)),
            scratch_shapes=[
                pltpu.VMEM((2, own_rows, cycle_size), jnp.float32),
                pltpu.VMEM((2, own_rows, cycle_size), jnp.float32),
            ],
            compiler_params=PARAMS,
        )(scalars, queries, new_cycle, sinks)
        for part in range(parts)
    ]

    groups = {"a": slice(2 * own_rows, new_count), "b": slice(0, 2 * own_rows)}

    def halves(rows):
        size = (rows.stop - rows.start) // 2
        return (jax.ShapeDtypeStruct((size, model_width), jnp.bfloat16),) * 2

    def mix():
        return pl.pallas_call(
            functools.partial(mix_kernel, out_spots, len(out_arrays), parts, own_rows),
            out_shape=halves(slice(0, new_count)),
            in_specs=[SMEM] + [VMEM] * (parts + len(out_arrays)),
            out_specs=(VMEM, VMEM),
            scratch_shapes=[pltpu.VMEM((model_width, local_cols), jnp.bfloat16)],
            compiler_params=PARAMS,
            name="mix",
        )(scalars, *attended, *out_arrays)

    sums = jnp.split(here.core_sum(mix()).astype(jnp.bfloat16), nx)
    totals = [[part] for part in sums]
    for step in range(1, nx):
        for d in reversed(range(nx)):
            moved = here.to_x(sums[d], step)
            totals[(d + step) % nx].append(moved)

    def norm(base, row, terms, name):
        return pl.pallas_call(
            functools.partial(norm_kernel, row),
            out_shape=jax.ShapeDtypeStruct(base.shape, jnp.bfloat16),
            in_specs=[VMEM] * (2 + len(terms)),
            out_specs=VMEM,
            compiler_params=LIGHT if name == "last" else PARAMS,
        )(base, alphas, *terms)

    after = []
    after_blocks = []
    for d in range(nx):
        after.append(norm(row_blocks[2 * d], 0, totals[d], f"norm{d}"))
        after_blocks += [after[d], here.swap_core(after[d])]

    tile = 256 if units % 256 == 0 else 128
    piece_rows = gated_arrays[0].shape[1]
    active = pl.pallas_call(
        functools.partial(units_kernel, gated_spots, len(gated_arrays), blocks),
        grid=(units // tile,),
        out_shape=jax.ShapeDtypeStruct((new_count, units), jnp.bfloat16),
        in_specs=[SMEM]
        + [pl.BlockSpec((2, tile), lambda n: (0, n))]
        + [pl.BlockSpec((2, piece_rows, tile), lambda n: (0, 0, n))] * len(gated_arrays)
        + [pl.BlockSpec((own_rows, model_width), lambda n: (0, 0))] * blocks,
        out_specs=pl.BlockSpec((new_count, tile), lambda n: (0, n)),
        scratch_shapes=[pltpu.VMEM((2, model_width, tile), jnp.bfloat16)],
        compiler_params=PARAMS,
        name="units",
    )(scalars, scales, *gated_arrays, *after_blocks)

    down_arrays = [*first_arrays, *second_arrays]

    def lower(group):
        rows = groups[group]
        counts = (len(first_arrays), len(second_arrays))
        return pl.pallas_call(
            functools.partial(lower_kernel, (first_spots, second_spots), counts, own_rows, rows),
            out_shape=halves(rows),
            in_specs=[SMEM] + [VMEM] * (1 + len(down_arrays)),
            out_specs=(VMEM, VMEM),
            scratch_shapes=[pltpu.VMEM((model_width, units), jnp.bfloat16)],
            compiler_params=LIGHT,
        )(scalars, active, *down_arrays)

    far = jnp.split(here.core_sum(lower("a")).astype(jnp.bfloat16), nx - 1)
    kept, sent = lower("b")
    terms = [kept, here.swap_core(sent)]
    terms += [here.to_x(far[d - 1], -d) for d in range(1, nx)]
    result = norm(after[0], 1, terms, "last")
    return (result[None], new_cycle[None])


def solution(mesh):
    axes = (mesh.shape["gx"], mesh.shape["gy"])

    def body(*args):
        return per_device(axes, *args)

    return jax.shard_map(
        body,
        mesh=mesh,
        in_specs=(
            P("gy", "gx", None),
            P("gy"),
            P("gy", None, None, "gx"),
            P("gy", None, None, "gx"),
            P("gy", None, "gx"),
            P("gx"),
            P("gx", "gy"),
            P(),
            P("gy", "gx"),
            P("gy", "gx"),
            P("gx"),
            P("gx"),
            P("gx", "gy"),
            P(),
        ),
        out_specs=(P("gy", "gx", None), P("gy", None, None, "gx")),
        check_vma=False,
    )
```
